256 devices in a mesh: sec: 8 (over z), row: 8 (over y_lo, x), inner: 4 (over y_hi, core).
Axes of the slice: x: 4, y: 4 (y_hi: 2, y_lo: 2; y = y_hi * 2 + y_lo), z: 8, core: 2. Of those that a mesh axis runs over, the one named last changes fastest.
Arguments:
- amplitudes: bfloat16 [1024, 4, 16384], P('row', 'inner'), may hold values from -6 to 6
- hole_ladder: bfloat16 [1024, 1024], P('row'), may hold values from -0.1875 to 0.1875
- bare_integrals: bfloat16 [1024, 4, 16384], P('row', 'inner', 'sec'), may hold values from -6 to 6
- ladder_tiles: bfloat16 [2048, 512, 128], P('sec', 'inner'), may hold values from -0.125 to 0.125
- ladder_source: int32 [2048, 4], P('sec', 'inner'), may hold values from 0 to 127
- ladder_target: int32 [2048, 4], P('sec', 'inner'), may hold values from 0 to 127
- ladder_live: int32 [8, 4], P('sec', 'inner'), may hold values from 64 to 256, as said below
- cycle_tiles: bfloat16 [256, 512, 128], P('sec', 'inner'), may hold values from -0.375 to 0.375
- cycle_source: int32 [256, 4], P('sec', 'inner'), may hold values from 0 to 63
- cycle_target: int32 [256, 4], P('sec', 'inner'), may hold values from 0 to 127
- gap_rows: int32 [1024], P('row'), may hold values from 512 to 2047
- gap_columns: int32 [4, 16384], P('inner', 'sec'), may hold values from 512 to 2047
Outputs:
- updated: bfloat16 [1024, 4, 16384], P('row', 'inner', 'sec')
The draws below stay inside these ranges and needn't reach their ends.
Inputs may be any that keep to these rules, and one draw needn't show every extreme that they name: Slots from ladder_live on are padding and carry no term; some section and quarter has all 256 slots live in every draw.
All inputs are finite; a program needn't handle non-finite values.
Results may differ from the reference program's by a relative error of at most 0.0095.
Values may be sent and summed in bfloat16 or wider, within the bound.
No kernel may reach another device: no remote copies, remote signals or barrier semaphores. Data moves between devices by JAX's collectives and lax.ppermute only.
A program may use at most 128 MiB of HBM per device.

```python
import jax
import jax.numpy as jnp

V_PAIRS = 65536
TILE = 128
PANEL = 2048
TILE_DEV = 256
CYCLE_DEV = 32
ROWS = 1024
QUARTER = 16384
QUARTER_BLOCKS = 128
PANEL_BLOCKS = 64
N_SEC = 8
N_INNER = 4


def draw_ladder_live(key, part):
    first_key, second_key = jax.random.split(jax.random.fold_in(key, 17))
    counts = jax.random.randint(first_key, (N_SEC * N_INNER,), TILE_DEV // 4, TILE_DEV + 1)
    chosen = jax.random.randint(second_key, (), 0, N_SEC * N_INNER)
    counts = jnp.where(jnp.arange(N_SEC * N_INNER) == chosen, TILE_DEV, counts)
    return counts.reshape(N_SEC, N_INNER).astype(jnp.int32)


def set_ends(values, own_key, least, high):
    dims = values.shape
    index_at = [jax.random.randint(jax.random.fold_in(own_key, axis), (), 0, dims[axis]) for axis in range(len(dims))]
    values = values.at[tuple(index_at)].set(least)
    longest = dims.index(max(dims))
    index_at[longest] = (index_at[longest] + 1) % dims[longest]
    return values.at[tuple(index_at)].set(high)


def level_of(own_key, extent, pieces, smallest, top_value):
    level = 1.0
    for axis_at, parts in pieces:
        heights = jax.random.uniform(jax.random.fold_in(jax.random.fold_in(own_key, 6), axis_at), (parts,), jnp.float32, smallest / len(pieces), top_value / len(pieces))
        level = level * jnp.repeat(jnp.exp(heights), extent[axis_at] // parts).reshape((-1,) + (1,) * (len(extent) - 1 - axis_at))
    return level


def gaussian(own_key, dims, scale, bound, cuts=(), held_as=jnp.bfloat16):
    drawn = jax.random.normal(own_key, dims, jnp.float32) * scale
    if len(cuts) > 0:
        drawn = level_of(own_key, dims, cuts, -0.22, 0.18) * drawn
    return jnp.clip(drawn, min=-bound, max=bound).astype(held_as)


def setup_inputs(seed: int = 0) -> dict:
    key_list = jax.random.split(jax.random.key(seed), 13)
    return {
        "amplitudes": gaussian(key_list[0], (ROWS, N_INNER, QUARTER), 1.0, 6.0, ((0, 8), (1, 4))),
        "hole_ladder": gaussian(key_list[1], (ROWS, ROWS), ROWS ** -0.5, 0.1875, ((0, 8),)),
        "bare_integrals": gaussian(key_list[2], (ROWS, N_INNER, QUARTER), 1.0, 6.0, ((0, 8), (1, 4), (2, 8))),
        "ladder_tiles": gaussian(key_list[3], (N_SEC * TILE_DEV, N_INNER * TILE, TILE), (TILE * max(1, N_SEC * TILE_DEV // QUARTER_BLOCKS)) ** -0.5, 0.125, ((0, 8), (1, 4))),
        "ladder_source": set_ends(jax.random.randint(key_list[4], (N_SEC * TILE_DEV, N_INNER), 0, QUARTER_BLOCKS), jax.random.fold_in(key_list[4], 1), 0, QUARTER_BLOCKS - 1).astype(jnp.int32),
        "ladder_target": set_ends(jax.random.randint(key_list[5], (N_SEC * TILE_DEV, N_INNER), 0, QUARTER_BLOCKS), jax.random.fold_in(key_list[5], 1), 0, QUARTER_BLOCKS - 1).astype(jnp.int32),
        "ladder_live": draw_ladder_live(jax.random.fold_in(key_list[12], 71), 0),
        "cycle_tiles": gaussian(key_list[7], (N_SEC * CYCLE_DEV, N_INNER * TILE, TILE), (TILE * max(1, N_SEC * CYCLE_DEV // QUARTER_BLOCKS)) ** -0.5, 0.375, ((0, 8), (1, 4))),
        "cycle_source": set_ends(jax.random.randint(key_list[8], (N_SEC * CYCLE_DEV, N_INNER), 0, PANEL_BLOCKS), jax.random.fold_in(key_list[8], 1), 0, PANEL_BLOCKS - 1).astype(jnp.int32),
        "cycle_target": set_ends(jax.random.randint(key_list[9], (N_SEC * CYCLE_DEV, N_INNER), 0, QUARTER_BLOCKS), jax.random.fold_in(key_list[9], 1), 0, QUARTER_BLOCKS - 1).astype(jnp.int32),
        "gap_rows": set_ends(jax.random.randint(key_list[10], (ROWS,), 512, 2048), jax.random.fold_in(key_list[10], 1), 512, 2047).astype(jnp.int32),
        "gap_columns": set_ends(jax.random.randint(key_list[11], (N_INNER, QUARTER), 512, 2048), jax.random.fold_in(key_list[11], 1), 512, 2047).astype(jnp.int32),
    }


def tile_term(source_blocks, tiles, sources, targets, live_count, block_count):
    tile_count = tiles.shape[0]
    picked = jnp.take(source_blocks, sources, axis=1)
    contribution = jnp.einsum("rtk,tkc->rtc", picked.astype(jnp.float32), tiles.astype(jnp.float32))
    keep_mask = (jnp.arange(tile_count) < live_count).astype(jnp.float32)
    contribution = contribution * keep_mask[None, :, None]
    totals = jnp.zeros((source_blocks.shape[0], block_count, TILE), jnp.float32)
    return totals.at[:, targets].add(contribution)


def reference(amplitudes, hole_ladder, bare_integrals, ladder_tiles, ladder_source, ladder_target, ladder_live, cycle_tiles, cycle_source, cycle_target, gap_rows, gap_columns):
    quarter_width = V_PAIRS // N_INNER
    block_count = quarter_width // TILE
    panel = amplitudes[:, :, :PANEL].reshape(ROWS, N_INNER * PANEL // TILE, TILE)
    quarters = []
    for quarter in range(N_INNER):
        own_blocks = amplitudes[:, quarter, :].reshape(ROWS, block_count, TILE)
        residual = bare_integrals[:, quarter, :].astype(jnp.float32)
        residual = residual + jnp.dot(hole_ladder, amplitudes[:, quarter, :], preferred_element_type=jnp.float32)
        for section in range(N_SEC):
            ladder_slots = slice(section * TILE_DEV, (section + 1) * TILE_DEV)
            cycle_slots = slice(section * CYCLE_DEV, (section + 1) * CYCLE_DEV)
            tile_rows = slice(quarter * TILE, (quarter + 1) * TILE)
            ladder_part = tile_term(own_blocks, ladder_tiles[ladder_slots, tile_rows, :], ladder_source[ladder_slots, quarter], ladder_target[ladder_slots, quarter], ladder_live[section, quarter], block_count)
            cycle_part = tile_term(panel, cycle_tiles[cycle_slots, tile_rows, :], cycle_source[cycle_slots, quarter], cycle_target[cycle_slots, quarter], CYCLE_DEV, block_count)
            share = (ladder_part + cycle_part).reshape(ROWS, quarter_width).astype(jnp.bfloat16)
            residual = residual + share.astype(jnp.float32)
        denominator = (gap_rows[:, None] + gap_columns[quarter][None, :]).astype(jnp.float32) / 1024.0
        quarters.append((residual / denominator).astype(jnp.bfloat16))
    return jnp.stack(quarters, axis=1)
```

```python
import functools

import jax
import jax.numpy as jnp
from jax import lax
from jax.experimental import pallas as pl
from jax.experimental.pallas import tpu as pltpu
from jax.sharding import PartitionSpec as P

TILE = 128
PANEL = 2048
VMEM = pltpu.VMEM
F32 = jnp.float32
BF16 = jnp.bfloat16


def whole(memory_space=VMEM):
    return pl.BlockSpec(memory_space=memory_space)


def ladder_body(source, target, live, amps, tiles, low, high, *, per_step, unroll):
    step = pl.program_id(0)
    trash = low.shape[0] - 1
    half = low.shape[1]

    @pl.when(step == 0)
    def _():
        @pl.loop(0, trash // 8)
        def _(block):
            zero = jnp.zeros((8, half, TILE), F32)
            low[pl.ds(block * 8, 8)] = zero
            high[pl.ds(block * 8, 8)] = zero

    base = step * per_step
    count = jnp.clip(live[0] - base, 0, per_step)

    def group(turn, carry):
        products = []
        for k in range(unroll):
            slot = turn * unroll + k
            start = pl.multiple_of(source[base + slot] * TILE, TILE)
            products.append(
                jnp.dot(amps[:, pl.ds(start, TILE)], tiles[slot], preferred_element_type=F32)
            )
        for k in range(unroll):
            slot = base + turn * unroll + k
            into = jnp.where(slot < live[0], target[slot], trash)
            low[into] += products[k][:half]
            high[into] += products[k][half:]
        return carry

    lax.fori_loop(0, (count + unroll - 1) // unroll, group, 0)


def ladder(amps, tiles, source, target, live, *, per_step=32, unroll=16):
    rows, width = amps.shape
    slots = tiles.shape[0]
    acc = jax.ShapeDtypeStruct((width // TILE + 1, rows // 2, TILE), F32)
    grid_spec = pltpu.PrefetchScalarGridSpec(
        num_scalar_prefetch=3,
        grid=(slots // per_step,),
        in_specs=[whole(), pl.BlockSpec((per_step, TILE, TILE), lambda g, *_: (g, 0, 0))],
        out_specs=[whole(), whole()],
    )
    return pl.pallas_call(
        functools.partial(ladder_body, per_step=per_step, unroll=unroll),
        out_shape=(acc, acc),
        grid_spec=grid_spec,
        name="ladder",
        compiler_params=pltpu.CompilerParams(vmem_limit_bytes=20 << 20),
        cost_estimate=pl.CostEstimate(
            flops=2 * slots * rows * TILE * TILE, bytes_accessed=24 << 20, transcendentals=0
        ),
    )(source, target, live, amps, tiles)


def cycle_body(
    source, target, place, acc_in, own, near, far, both, tiles, acc, *outs, half_at, unroll
):
    rows = acc.shape[1]
    panels = outs[-1]
    shares = outs[:-1]
    per_panel = own.shape[1] // TILE
    blocks = shares[0].shape[0]
    n_sec = (acc.shape[0] - 1) // blocks
    panels[0] = own[...]
    panels[1] = near[pl.ds(half_at, rows), :]
    panels[2] = far[...]
    panels[3] = both[...]

    def group(turn, carry):
        products = []
        for k in range(unroll):
            slot = turn * unroll + k
            block = source[slot]
            which = (block // per_panel) ^ place[1]
            start = pl.multiple_of((block % per_panel) * TILE, TILE)
            products.append(
                jnp.dot(
                    panels[which, :, pl.ds(start, TILE)],
                    tiles[slot],
                    preferred_element_type=F32,
                )
            )
        for k in range(unroll):
            acc[target[turn * unroll + k]] += products[k]
        return carry

    lax.fori_loop(0, tiles.shape[0] // unroll, group, 0)
    for k in range(n_sec):
        chunk = lax.rem(place[0] + k, n_sec) * blocks
        shares[k][...] = acc[pl.ds(chunk, blocks)].astype(BF16)


def cycle(acc, own, near, far, both, tiles, source, target, place, *, half_at, n_sec, unroll=16):
    rows = acc.shape[1]
    blocks = (acc.shape[0] - 1) // n_sec
    share = jax.ShapeDtypeStruct((blocks, rows, TILE), BF16)
    grid_spec = pltpu.PrefetchScalarGridSpec(
        num_scalar_prefetch=3,
        grid=(),
        in_specs=[whole()] * 6,
        out_specs=[whole()] * (1 + n_sec),
        scratch_shapes=[VMEM((4, rows, own.shape[1]), BF16)],
    )
    outs = pl.pallas_call(
        functools.partial(cycle_body, half_at=half_at, unroll=unroll),
        out_shape=(jax.ShapeDtypeStruct(acc.shape, F32),) + (share,) * n_sec,
        grid_spec=grid_spec,
        input_output_aliases={3: 0},
        name="cycle",
        compiler_params=pltpu.CompilerParams(vmem_limit_bytes=20 << 20),
        cost_estimate=pl.CostEstimate(
            flops=2 * tiles.shape[0] * rows * TILE * TILE, bytes_accessed=6 << 20, transcendentals=0
        ),
    )(source, target, place, acc, own, near, far, both, tiles)
    return outs[1:]


def hole_body(place, hole, partner, block_0, block_1, block_2, block_3, own_out, partner_out):
    line, x_at, line_size = place[2], place[3], 4
    for which, out in ((partner, partner_out), (hole, own_out)):
        total = None
        for d, block in enumerate((block_0, block_1, block_2, block_3)):
            column = lax.rem(x_at + d, line_size)
            if which is hole:
                column = column + line * line_size
            start = pl.multiple_of(column * TILE, TILE)
            term = jnp.dot(
                which[:, pl.ds(start, TILE)], block[...], preferred_element_type=F32
            )
            total = term if total is None else total + term
        out[...] = total.astype(out.dtype)


def hole_products(hole, partner, blocks, place):
    rows, width = blocks[0].shape
    columns = 512
    block_spec = pl.BlockSpec((rows, columns), lambda c, *_: (0, c))
    grid_spec = pltpu.PrefetchScalarGridSpec(
        num_scalar_prefetch=1,
        grid=(width // columns,),
        in_specs=[
            pl.BlockSpec(hole.shape, lambda c, *_: (0, 0)),
            pl.BlockSpec(partner.shape, lambda c, *_: (0, 0)),
        ]
        + [block_spec] * 4,
        out_specs=[block_spec, block_spec],
    )
    return pl.pallas_call(
        hole_body,
        out_shape=(
            jax.ShapeDtypeStruct((rows, width), F32),
            jax.ShapeDtypeStruct((rows, width), BF16),
        ),
        grid_spec=grid_spec,
        name="hole",
        compiler_params=pltpu.CompilerParams(vmem_limit_bytes=16 << 20),
        cost_estimate=pl.CostEstimate(
            flops=2 * 2 * rows * 4 * rows * width, bytes_accessed=5 << 20, transcendentals=0
        ),
    )(place, hole, partner, *blocks)


def last_body(gap_rows, gap_columns, bare, hole_own, hole_partner, *refs):
    out = refs[-1]
    shares = refs[:-1]
    half = shares[0].shape[1]
    for b in range(shares[0].shape[0]):
        cols = slice(b * TILE, (b + 1) * TILE)
        base = bare[:, cols].astype(F32) + hole_own[:, cols] + hole_partner[:, cols].astype(F32)
        gap = (gap_rows[...] + gap_columns[:, cols]).astype(F32) / 1024.0
        for u in range(2):
            at = slice(u * half, (u + 1) * half)
            own, forward, backward = shares[3 * u : 3 * u + 3]
            joined = own[b].astype(F32) + forward[b].astype(F32) + backward[b].astype(F32)
            out[at, cols] = ((base[at] + joined) / gap[at]).astype(out.dtype)


def last(gap_rows, gap_columns, bare, hole_own, hole_partner, shares):
    rows, width = bare.shape
    steps = 4
    columns = width // steps
    half = shares[0].shape[1]
    wide = pl.BlockSpec((rows, columns), lambda c: (0, c))
    share = pl.BlockSpec((columns // TILE, half, TILE), lambda c: (c, 0, 0))
    return pl.pallas_call(
        last_body,
        out_shape=jax.ShapeDtypeStruct((rows, width), BF16),
        grid=(steps,),
        in_specs=[
            pl.BlockSpec((rows, 1), lambda c: (0, 0)),
            pl.BlockSpec((1, columns), lambda c: (0, c)),
            wide,
            wide,
            wide,
        ]
        + [share] * 6,
        out_specs=wide,
        name="last",
        compiler_params=pltpu.CompilerParams(vmem_limit_bytes=16 << 20),
        cost_estimate=pl.CostEstimate(flops=10 * rows * width, bytes_accessed=5 << 20, transcendentals=0),
    )(gap_rows, gap_columns, bare, hole_own, hole_partner, *shares)


def per_device(
    amplitudes,
    hole_ladder,
    bare_integrals,
    ladder_tiles,
    ladder_source,
    ladder_target,
    ladder_live,
    cycle_tiles,
    cycle_source,
    cycle_target,
    gap_rows,
    gap_columns,
    *,
    n_sec,
):
    rows = amplitudes.shape[0]
    half = rows // 2
    owned = bare_integrals.shape[2]
    amps = amplitudes.reshape(rows, amplitudes.shape[2])
    sec = lax.axis_index("sec")
    row = lax.axis_index("row")
    place = jnp.stack([sec, lax.axis_index("inner"), row // 4, row % 4]).astype(jnp.int32)

    forward = [(i, (i + 1) % n_sec) for i in range(n_sec)]
    backward = [(i, (i - 1) % n_sec) for i in range(n_sec)]
    core_flip = [(i, i ^ 1) for i in range(4)]
    y_flip = [(i, i ^ 2) for i in range(4)]
    row_flip = [(i, i ^ 4) for i in range(8)]
    x_next = [(i, (i & 4) + (i + 1) % 4) for i in range(8)]
    x_back = [(i, (i & 4) + (i + 3) % 4) for i in range(8)]
    x_over = [(i, (i & 4) + (i + 2) % 4) for i in range(8)]

    own_panel = [amps[u * half : (u + 1) * half, :PANEL] for u in range(2)]
    far = [lax.ppermute(p, "inner", y_flip) for p in own_panel]
    near = lax.ppermute(amps[:, :PANEL], "inner", core_flip)
    both = [lax.ppermute(p, "inner", core_flip) for p in far]

    mine = lax.dynamic_slice_in_dim(amps, sec * owned, owned, 1)
    behind = lax.ppermute(mine, "row", x_next)
    ahead = lax.ppermute(mine, "row", x_back)
    over = lax.ppermute(mine, "row", x_over)
    other_columns = lax.dynamic_slice_in_dim(
        hole_ladder, (1 - row // 4) * (4 * rows), 4 * rows, 1
    )
    partner_hole = lax.ppermute(other_columns, "row", row_flip)

    accs = ladder(
        amps,
        ladder_tiles,
        ladder_source[:, 0],
        ladder_target[:, 0],
        ladder_live[:, 0],
    )
    hole_own, partner_part = hole_products(
        hole_ladder, partner_hole, (mine, ahead, over, behind), place
    )
    hole_partner = lax.ppermute(partner_part, "row", row_flip)

    joined = []
    for u in range(2):
        shares = cycle(
            accs[u],
            own_panel[u],
            near,
            far[u],
            both[u],
            cycle_tiles,
            cycle_source[:, 0],
            cycle_target[:, 0],
            place,
            half_at=u * half,
            n_sec=n_sec,
        )
        reach = (n_sec // 2, n_sec // 2 - 1)
        ways = ((forward, reach[u], 1), (backward, reach[1 - u], -1))
        sums = []
        for way, hops, sign in ways:
            moving = shares[(sign * hops) % n_sec]
            for hop in range(hops - 1, -1, -1):
                moving = lax.ppermute(moving, "sec", way)
                if hop:
                    kept = shares[(sign * hop) % n_sec]
                    moving = (moving.astype(F32) + kept.astype(F32)).astype(BF16)
            sums.append(moving)
        joined += [shares[0]] + sums

    updated = last(
        gap_rows.reshape(rows, 1),
        gap_columns,
        bare_integrals.reshape(rows, owned),
        hole_own,
        hole_partner,
        joined,
    )
    return updated.reshape(rows, 1, owned)


def solution(mesh):
    in_specs = (
        P("row", "inner", None),
        P("row", None),
        P("row", "inner", "sec"),
        P("sec", "inner", None),
        P("sec", "inner"),
        P("sec", "inner"),
        P("sec", "inner"),
        P("sec", "inner", None),
        P("sec", "inner"),
        P("sec", "inner"),
        P("row"),
        P("inner", "sec"),
    )
    out_specs = P("row", "inner", "sec")
    return jax.shard_map(
        functools.partial(per_device, n_sec=mesh.shape["sec"]),
        mesh=mesh,
        in_specs=in_specs,
        out_specs=out_specs,
        check_vma=False,
    )
```

```python
import functools

import jax
import jax.numpy as jnp
from jax import lax
from jax.experimental import pallas as pl
from jax.experimental.pallas import tpu as pltpu
from jax.sharding import PartitionSpec as P


TILE = 128
PANEL = 2048
VMEM = pltpu.VMEM
F32 = jnp.float32
BF16 = jnp.bfloat16


def whole(memory_space=VMEM):
    return pl.BlockSpec(memory_space=memory_space)


def in_hbm(*arrays):
    return tuple(pltpu.with_memory_space_constraint(a, pltpu.HBM) for a in arrays)


def prepare_body(amps, hole, panel, mine, columns, sem):
    wide, narrow = mine.shape[1], columns.shape[1]
    at = pl.multiple_of(lax.axis_index("sec") * wide, wide)
    line = lax.axis_index("row") // 4
    line_at = pl.multiple_of((1 - line) * narrow, narrow)
    copies = [
        pltpu.make_async_copy(amps.at[:, pl.ds(0, panel.shape[1])], panel, sem.at[0]),
        pltpu.make_async_copy(amps.at[:, pl.ds(at, wide)], mine, sem.at[1]),
        pltpu.make_async_copy(hole.at[:, pl.ds(line_at, narrow)], columns, sem.at[2]),
    ]
    for copy in copies:
        copy.start()
    for copy in copies:
        copy.wait()


def prepare(amps, hole, owned):
    rows = amps.shape[0]
    return pl.pallas_call(
        prepare_body,
        out_shape=(
            jax.ShapeDtypeStruct((rows, PANEL), BF16),
            jax.ShapeDtypeStruct((rows, owned), BF16),
            jax.ShapeDtypeStruct((rows, 4 * rows), BF16),
        ),
        in_specs=[whole(pltpu.HBM)] * 2,
        out_specs=[whole()] * 3,
        scratch_shapes=[pltpu.SemaphoreType.DMA((3,))],
        name="prepare",
        compiler_params=pltpu.CompilerParams(vmem_limit_bytes=4 << 20),
        cost_estimate=pl.CostEstimate(flops=0, bytes_accessed=3 << 20, transcendentals=0),
    )(*in_hbm(amps, hole))


def tile_group(turn, unroll, block_of, tiles, acc, into_of):
    products = []
    for k in range(unroll):
        slot = turn * unroll + k
        products.append(jnp.dot(block_of(slot), tiles[slot], preferred_element_type=F32))
    for k in range(unroll):
        acc[into_of(turn * unroll + k)] += products[k]


def ladder_body(
    source_at, target_at, live_at, amps_at, tiles_at, acc,
    source, target, live, amps, tiles, index_sem, amps_sem, tile_sem, *, parts, unroll,
):
    per_part = tiles.shape[0] // parts
    trash = acc.shape[0] - 1
    copies = [
        pltpu.make_async_copy(at, ref, index_sem.at[k])
        for k, (at, ref) in enumerate(
            ((source_at, source), (target_at, target), (live_at, live))
        )
    ]
    pieces = amps_sem.shape[0]
    height = amps.shape[0] // pieces
    for k in range(pieces):
        at = pl.ds(k * height, height)
        copies.append(pltpu.make_async_copy(amps_at.at[at], amps.at[at], amps_sem.at[k]))
    for copy in copies:
        copy.start()

    def tile_copy(part):
        slots = pl.ds(part * per_part, per_part)
        return pltpu.make_async_copy(tiles_at.at[slots], tiles.at[slots], tile_sem.at[part])

    tile_copy(0).start()

    @pl.loop(0, trash // 8)
    def _(block):
        acc[pl.ds(block * 8, 8)] = jnp.zeros((8,) + acc.shape[1:], F32)

    for copy in copies:
        copy.wait()
    for part in range(1, parts):
        tile_copy(part).start()

    def block_of(slot):
        return amps[:, pl.ds(pl.multiple_of(source[slot] * TILE, TILE), TILE)]

    def into_of(slot):
        return jnp.where(slot < live[0], target[slot], trash)

    for part in range(parts):
        tile_copy(part).wait()
        first = part * per_part // unroll
        count = jnp.clip(live[0] - part * per_part, 0, per_part)

        def group(turn, carry):
            tile_group(turn, unroll, block_of, tiles, acc, into_of)
            return carry

        lax.fori_loop(first, first + (count + unroll - 1) // unroll, group, 0)


def ladder(amps, tiles, source, target, live, *, parts=8, unroll=16):
    rows, width = amps.shape
    slots = tiles.shape[0]
    return pl.pallas_call(
        functools.partial(ladder_body, parts=parts, unroll=unroll),
        out_shape=jax.ShapeDtypeStruct((width // TILE + 1, rows, TILE), F32),
        in_specs=[whole(pltpu.HBM)] * 5,
        out_specs=whole(),
        scratch_shapes=[
            pltpu.SMEM(source.shape, jnp.int32),
            pltpu.SMEM(target.shape, jnp.int32),
            pltpu.SMEM(live.shape, jnp.int32),
            VMEM(amps.shape, BF16),
            VMEM(tiles.shape, BF16),
            pltpu.SemaphoreType.DMA((3,)),
            pltpu.SemaphoreType.DMA((4,)),
            pltpu.SemaphoreType.DMA((parts,)),
        ],
        name="ladder",
        compiler_params=pltpu.CompilerParams(vmem_limit_bytes=28 << 20),
        cost_estimate=pl.CostEstimate(
            flops=2 * slots * rows * TILE * TILE, bytes_accessed=12 << 20, transcendentals=0
        ),
    )(*in_hbm(source, target), live, *in_hbm(amps, tiles))


def cycle_body(
    source_at, target_at, _, own, near, far, both, tiles, acc, *rest, n_sec, unroll
):
    *shares, source, target, panels, index_sem, panel_sem = rest
    rows = acc.shape[1]
    per_panel = panels.shape[2] // TILE
    blocks, half, _ = shares[0].shape
    copies = [
        pltpu.make_async_copy(source_at, source, index_sem.at[0]),
        pltpu.make_async_copy(target_at, target, index_sem.at[1]),
    ]
    for k, panel in enumerate((own, near, far, both)):
        copies.append(pltpu.make_async_copy(panel, panels.at[k], panel_sem.at[k]))
    for copy in copies:
        copy.start()
    for copy in copies:
        copy.wait()
    sec, quarter = lax.axis_index("sec"), lax.axis_index("inner")

    def block_of(slot):
        block = source[slot]
        start = pl.multiple_of((block % per_panel) * TILE, TILE)
        return panels[(block // per_panel) ^ quarter, :, pl.ds(start, TILE)]

    def group(turn, carry):
        tile_group(turn, unroll, block_of, tiles, acc, lambda slot: target[slot])
        return carry

    lax.fori_loop(0, tiles.shape[0] // unroll, group, 0)
    for k in range(n_sec):
        chunk = lax.rem(sec + k, n_sec) * blocks
        for u in range(rows // half):
            at = pl.ds(u * half, half)
            shares[u * n_sec + k][...] = acc[pl.ds(chunk, blocks), at].astype(BF16)


def cycle(acc, own, near, far, both, tiles, source, target, *, n_sec, unroll=16):
    blocks = (acc.shape[0] - 1) // n_sec
    rows = acc.shape[1]
    share = jax.ShapeDtypeStruct((blocks, rows // 2, TILE), BF16)
    outs = pl.pallas_call(
        functools.partial(cycle_body, n_sec=n_sec, unroll=unroll),
        out_shape=(jax.ShapeDtypeStruct(acc.shape, F32),) + (share,) * (2 * n_sec),
        in_specs=[whole(pltpu.HBM)] * 2 + [whole()] + [whole(pl.ANY)] * 4 + [whole()],
        out_specs=[whole()] * (1 + 2 * n_sec),
        scratch_shapes=[
            pltpu.SMEM(source.shape, jnp.int32),
            pltpu.SMEM(target.shape, jnp.int32),
            VMEM((4, rows, PANEL), BF16),
            pltpu.SemaphoreType.DMA((2,)),
            pltpu.SemaphoreType.DMA((4,)),
        ],
        input_output_aliases={2: 0},
        name="cycle",
        compiler_params=pltpu.CompilerParams(vmem_limit_bytes=24 << 20),
        cost_estimate=pl.CostEstimate(
            flops=2 * tiles.shape[0] * rows * TILE * TILE, bytes_accessed=6 << 20, transcendentals=0
        ),
    )(*in_hbm(source, target), acc, own, near, far, both, tiles)
    return outs[1 : 1 + n_sec], outs[1 + n_sec :]


def join_body(moving, kept, out):
    out[...] = (moving[...].astype(F32) + kept[...].astype(F32)).astype(out.dtype)


def join(moving, kept):
    return pl.pallas_call(
        join_body,
        out_shape=jax.ShapeDtypeStruct(moving.shape, moving.dtype),
        in_specs=[whole()] * 2,
        out_specs=whole(),
        name="join",
        compiler_params=pltpu.CompilerParams(vmem_limit_bytes=4 << 20),
        cost_estimate=pl.CostEstimate(flops=moving.size, bytes_accessed=3 << 18, transcendentals=0),
    )(moving, kept)


def hole_body(
    hole_at, partner_at, block_0, block_1, block_2, block_3, own_out, partner_out,
    left, line, small_sem, block_sem,
):
    rows = own_out.shape[0]
    depth = left.shape[1]
    line_size = depth // rows
    row = lax.axis_index("row")
    columns = pl.ds(pl.multiple_of((row // line_size) * depth, depth), depth)
    copies = [
        pltpu.make_async_copy(hole_at.at[:, columns], left.at[pl.ds(0, rows)], small_sem.at[0]),
        pltpu.make_async_copy(partner_at, left.at[pl.ds(rows, rows)], small_sem.at[1]),
    ]
    for d, block in enumerate((block_0, block_1, block_2, block_3)):
        at = pl.multiple_of(lax.rem(row + d, line_size) * rows, rows)
        copies.append(pltpu.make_async_copy(block, line.at[pl.ds(at, rows)], block_sem.at[d]))
    for copy in copies:
        copy.start()
    for copy in copies:
        copy.wait()
    step = 256

    @pl.loop(0, line.shape[1] // step)
    def _(turn):
        cols = pl.ds(pl.multiple_of(turn * step, step), step)
        both = jnp.dot(left[...], line[:, cols], preferred_element_type=F32)
        own_out[:, cols] = both[:rows]
        partner_out[:, cols] = both[rows:].astype(partner_out.dtype)


def hole_products(hole, partner, blocks):
    rows, width = blocks[0].shape
    return pl.pallas_call(
        hole_body,
        out_shape=(
            jax.ShapeDtypeStruct((rows, width), F32),
            jax.ShapeDtypeStruct((rows, width), BF16),
        ),
        in_specs=[whole(pltpu.HBM)] + [whole(pl.ANY)] * 5,
        out_specs=[whole(), whole()],
        scratch_shapes=[
            VMEM((2 * rows, partner.shape[1]), BF16),
            VMEM((4 * rows, width), BF16),
            pltpu.SemaphoreType.DMA((2,)),
            pltpu.SemaphoreType.DMA((4,)),
        ],
        name="hole",
        compiler_params=pltpu.CompilerParams(vmem_limit_bytes=10 << 20),
        cost_estimate=pl.CostEstimate(
            flops=2 * 2 * rows * 4 * rows * width, bytes_accessed=4 << 20, transcendentals=0
        ),
    )(*in_hbm(hole), partner, *blocks)


def base_body(
    gap_rows, gap_columns, bare, hole_own, hole_partner, low_own, low_joined, high_own, high_joined,
    out, scale,
):
    half = low_own.shape[1]
    down = jnp.broadcast_to(gap_rows[...].astype(F32), (out.shape[0], out.shape[0])).T
    for b in range(low_own.shape[0]):
        cols = slice(b * TILE, (b + 1) * TILE)
        scale[:, cols] = 1024.0 / (down + gap_columns[:, cols].astype(F32))
        both = bare[:, cols].astype(F32) + hole_own[:, cols] + hole_partner[:, cols].astype(F32)
        for u, own, joined in ((0, low_own, low_joined), (1, high_own, high_joined)):
            at = slice(u * half, (u + 1) * half)
            out[at, cols] = both[at] + own[b].astype(F32) + joined[b].astype(F32)


def base_sum(gap_rows, gap_columns, bare, hole_own, hole_partner, shares):
    rows, width = bare.shape
    out = jax.ShapeDtypeStruct((rows, width), F32)
    return pl.pallas_call(
        base_body,
        out_shape=(out, out),
        in_specs=[whole()] * 9,
        out_specs=[whole()] * 2,
        name="base",
        compiler_params=pltpu.CompilerParams(vmem_limit_bytes=10 << 20),
        cost_estimate=pl.CostEstimate(flops=5 * rows * width, bytes_accessed=4 << 20, transcendentals=0),
    )(gap_rows, gap_columns, bare, hole_own, hole_partner, *shares)


def last_body(base, scale, low, high, out_at, out, sem):
    blocks, half, _ = low.shape
    pieces = sem.shape[0]
    copies = []
    for piece in range(pieces):
        for b in range(piece * blocks // pieces, (piece + 1) * blocks // pieces):
            cols = slice(b * TILE, (b + 1) * TILE)
            for u, joined in ((0, low), (1, high)):
                at = slice(u * half, (u + 1) * half)
                residual = base[at, cols] + joined[b].astype(F32)
                out[at, cols] = (residual * scale[at, cols]).astype(out.dtype)
        width = out.shape[1] // pieces
        part = pl.ds(piece * width, width)
        copies.append(pltpu.make_async_copy(out.at[:, part], out_at.at[:, part], sem.at[piece]))
        copies[-1].start()
    for copy in copies:
        copy.wait()


def last(base, scale, low, high, *, pieces=4):
    rows, width = base.shape
    return pl.pallas_call(
        last_body,
        out_shape=jax.ShapeDtypeStruct((rows, width), BF16),
        in_specs=[whole()] * 4,
        out_specs=whole(pltpu.HBM),
        scratch_shapes=[VMEM((rows, width), BF16), pltpu.SemaphoreType.DMA((pieces,))],
        name="last",
        compiler_params=pltpu.CompilerParams(vmem_limit_bytes=8 << 20),
        cost_estimate=pl.CostEstimate(flops=3 * rows * width, bytes_accessed=3 << 20, transcendentals=0),
    )(base, scale, low, high)


def per_device(
    amplitudes,
    hole_ladder,
    bare_integrals,
    ladder_tiles,
    ladder_source,
    ladder_target,
    ladder_live,
    cycle_tiles,
    cycle_source,
    cycle_target,
    gap_rows,
    gap_columns,
    *,
    n_sec,
):
    rows = amplitudes.shape[0]
    owned = bare_integrals.shape[2]
    amps = amplitudes.reshape(rows, amplitudes.shape[2])

    forward = [(i, (i + 1) % n_sec) for i in range(n_sec)]
    backward = [(i, (i - 1) % n_sec) for i in range(n_sec)]
    core_flip = [(i, i ^ 1) for i in range(4)]
    y_flip = [(i, i ^ 2) for i in range(4)]
    row_flip = [(i, i ^ 4) for i in range(8)]
    x_next = [(i, (i & 4) + (i + 1) % 4) for i in range(8)]
    x_back = [(i, (i & 4) + (i + 3) % 4) for i in range(8)]
    x_over = [(i, (i & 4) + (i + 2) % 4) for i in range(8)]

    panel, mine, columns = prepare(amps, hole_ladder, owned)
    far = lax.ppermute(panel, "inner", y_flip)
    near = lax.ppermute(panel, "inner", core_flip)
    both = lax.ppermute(far, "inner", core_flip)
    behind = lax.ppermute(mine, "row", x_next)
    ahead = lax.ppermute(mine, "row", x_back)
    over = lax.ppermute(mine, "row", x_over)
    partner_columns = lax.ppermute(columns, "row", row_flip)

    acc = ladder(amps, ladder_tiles, ladder_source[:, 0], ladder_target[:, 0], ladder_live[:, 0])
    shares = cycle(
        acc,
        panel,
        near,
        far,
        both,
        cycle_tiles,
        cycle_source[:, 0],
        cycle_target[:, 0],
        n_sec=n_sec,
    )
    hole_own, partner_part = hole_products(
        hole_ladder, partner_columns, (mine, ahead, over, behind)
    )
    hole_partner = lax.ppermute(partner_part, "row", row_flip)

    ends = {}
    for u in range(2):
        reach = (n_sec // 2, n_sec // 2 - 1)
        ways = (("F", forward, reach[u], 1), ("B", backward, reach[1 - u], -1))
        for name, way, hops, sign in ways:
            moving = shares[u][(sign * hops) % n_sec]
            for hop in range(hops - 1, -1, -1):
                moving = lax.ppermute(moving, "sec", way)
                if hop:
                    moving = join(moving, shares[u][(sign * hop) % n_sec])
            ends[f"{name}{u}"] = moving

    base, scale = base_sum(
        gap_rows.reshape(1, rows),
        gap_columns,
        bare_integrals.reshape(rows, owned),
        hole_own,
        hole_partner,
        (shares[0][0], ends["B0"], shares[1][0], ends["F1"]),
    )
    updated = last(base, scale, ends["F0"], ends["B1"])
    return updated.reshape(rows, 1, owned)


def solution(mesh):
    in_specs = (
        P("row", "inner", None),
        P("row", None),
        P("row", "inner", "sec"),
        P("sec", "inner", None),
        P("sec", "inner"),
        P("sec", "inner"),
        P("sec", "inner"),
        P("sec", "inner", None),
        P("sec", "inner"),
        P("sec", "inner"),
        P("row"),
        P("inner", "sec"),
    )
    out_specs = P("row", "inner", "sec")
    return jax.shard_map(
        functools.partial(per_device, n_sec=mesh.shape["sec"]),
        mesh=mesh,
        in_specs=in_specs,
        out_specs=out_specs,
        check_vma=False,
    )
```

```python
import functools

import jax
import jax.numpy as jnp
from jax import lax
from jax.experimental import pallas as pl
from jax.experimental.pallas import tpu as pltpu
from jax.sharding import PartitionSpec as P


TILE = 128
PANEL = 2048
VMEM = pltpu.VMEM
F32 = jnp.float32
BF16 = jnp.bfloat16


def whole(memory_space=VMEM):
    return pl.BlockSpec(memory_space=memory_space)


def in_hbm(*arrays):
    return tuple(pltpu.with_memory_space_constraint(a, pltpu.HBM) for a in arrays)


def prepare_body(amps, hole, panel, mine, columns, sem):
    wide, narrow = mine.shape[1], columns.shape[1]
    at = pl.multiple_of(lax.axis_index("sec") * wide, wide)
    line = lax.axis_index("row") // 4
    line_at = pl.multiple_of((1 - line) * narrow, narrow)
    copies = [
        pltpu.make_async_copy(amps.at[:, pl.ds(0, panel.shape[1])], panel, sem.at[0]),
        pltpu.make_async_copy(amps.at[:, pl.ds(at, wide)], mine, sem.at[1]),
        pltpu.make_async_copy(hole.at[:, pl.ds(line_at, narrow)], columns, sem.at[2]),
    ]
    for copy in copies:
        copy.start()
    for copy in copies:
        copy.wait()


def prepare(amps, hole, owned):
    rows = amps.shape[0]
    return pl.pallas_call(
        prepare_body,
        out_shape=(
            jax.ShapeDtypeStruct((rows, PANEL), BF16),
            jax.ShapeDtypeStruct((rows, owned), BF16),
            jax.ShapeDtypeStruct((rows, 4 * rows), BF16),
        ),
        in_specs=[whole(pltpu.HBM)] * 2,
        out_specs=[whole()] * 3,
        scratch_shapes=[pltpu.SemaphoreType.DMA((3,))],
        name="prepare",
        compiler_params=pltpu.CompilerParams(vmem_limit_bytes=4 << 20),
        cost_estimate=pl.CostEstimate(flops=0, bytes_accessed=3 << 20, transcendentals=0),
    )(*in_hbm(amps, hole))


def tile_group(turn, unroll, block_of, tiles, acc, into_of):
    products = []
    for k in range(unroll):
        slot = turn * unroll + k
        products.append(jnp.dot(block_of(slot), tiles[slot], preferred_element_type=F32))
    for k in range(unroll):
        acc[into_of(turn * unroll + k)] += products[k]


def ladder_body(
    source_at, target_at, live_at, amps_at, tiles_at, acc,
    source, target, live, amps, tiles, index_sem, amps_sem, tile_sem, *, parts, unroll,
):
    per_part = tiles.shape[0] // parts
    trash = acc.shape[0] - 1
    copies = [
        pltpu.make_async_copy(at, ref, index_sem.at[k])
        for k, (at, ref) in enumerate(
            ((source_at, source), (target_at, target), (live_at, live))
        )
    ]
    pieces = amps_sem.shape[0]
    height = amps.shape[0] // pieces
    for k in range(pieces):
        at = pl.ds(k * height, height)
        copies.append(pltpu.make_async_copy(amps_at.at[at], amps.at[at], amps_sem.at[k]))
    for copy in copies:
        copy.start()

    def tile_copy(part):
        slots = pl.ds(part * per_part, per_part)
        return pltpu.make_async_copy(tiles_at.at[slots], tiles.at[slots], tile_sem.at[part])

    tile_copy(0).start()

    @pl.loop(0, trash // 8)
    def _(block):
        acc[pl.ds(block * 8, 8)] = jnp.zeros((8,) + acc.shape[1:], F32)

    for copy in copies:
        copy.wait()
    for part in range(1, parts):
        tile_copy(part).start()

    def block_of(slot):
        return amps[:, pl.ds(pl.multiple_of(source[slot] * TILE, TILE), TILE)]

    def into_of(slot):
        return jnp.where(slot < live[0], target[slot], trash)

    for part in range(parts):
        tile_copy(part).wait()
        first = part * per_part // unroll
        count = jnp.clip(live[0] - part * per_part, 0, per_part)

        def group(turn, carry):
            tile_group(turn, unroll, block_of, tiles, acc, into_of)
            return carry

        lax.fori_loop(first, first + (count + unroll - 1) // unroll, group, 0)


def ladder(amps, tiles, source, target, live, *, parts=8, unroll=16):
    rows, width = amps.shape
    slots = tiles.shape[0]
    return pl.pallas_call(
        functools.partial(ladder_body, parts=parts, unroll=unroll),
        out_shape=jax.ShapeDtypeStruct((width // TILE + 1, rows, TILE), F32),
        in_specs=[whole(pltpu.HBM)] * 5,
        out_specs=whole(),
        scratch_shapes=[
            pltpu.SMEM(source.shape, jnp.int32),
            pltpu.SMEM(target.shape, jnp.int32),
            pltpu.SMEM(live.shape, jnp.int32),
            VMEM(amps.shape, BF16),
            VMEM(tiles.shape, BF16),
            pltpu.SemaphoreType.DMA((3,)),
            pltpu.SemaphoreType.DMA((4,)),
            pltpu.SemaphoreType.DMA((parts,)),
        ],
        name="ladder",
        compiler_params=pltpu.CompilerParams(vmem_limit_bytes=28 << 20),
        cost_estimate=pl.CostEstimate(
            flops=2 * slots * rows * TILE * TILE, bytes_accessed=12 << 20, transcendentals=0
        ),
    )(*in_hbm(source, target), live, *in_hbm(amps, tiles))


def cycle_body(
    source_at, target_at, _, own, near, far, both, tiles, acc, *rest, n_sec, unroll
):
    *shares, source, target, panels, index_sem, panel_sem = rest
    rows = acc.shape[1]
    per_panel = panels.shape[2] // TILE
    blocks, half, _ = shares[0].shape
    copies = [
        pltpu.make_async_copy(source_at, source, index_sem.at[0]),
        pltpu.make_async_copy(target_at, target, index_sem.at[1]),
    ]
    for k, panel in enumerate((own, near, far, both)):
        copies.append(pltpu.make_async_copy(panel, panels.at[k], panel_sem.at[k]))
    for copy in copies:
        copy.start()
    for copy in copies:
        copy.wait()
    sec, quarter = lax.axis_index("sec"), lax.axis_index("inner")

    def block_of(slot):
        block = source[slot]
        start = pl.multiple_of((block % per_panel) * TILE, TILE)
        return panels[(block // per_panel) ^ quarter, :, pl.ds(start, TILE)]

    def group(turn, carry):
        tile_group(turn, unroll, block_of, tiles, acc, lambda slot: target[slot])
        return carry

    lax.fori_loop(0, tiles.shape[0] // unroll, group, 0)
    for k in range(n_sec):
        chunk = lax.rem(sec + k, n_sec) * blocks
        for u in range(rows // half):
            at = pl.ds(u * half, half)
            shares[u * n_sec + k][...] = acc[pl.ds(chunk, blocks), at].astype(BF16)


def cycle(acc, own, near, far, both, tiles, source, target, *, n_sec, unroll=16):
    blocks = (acc.shape[0] - 1) // n_sec
    rows = acc.shape[1]
    share = jax.ShapeDtypeStruct((blocks, rows // 2, TILE), BF16)
    outs = pl.pallas_call(
        functools.partial(cycle_body, n_sec=n_sec, unroll=unroll),
        out_shape=(jax.ShapeDtypeStruct(acc.shape, F32),) + (share,) * (2 * n_sec),
        in_specs=[whole(pltpu.HBM)] * 2 + [whole()] + [whole(pl.ANY)] * 4 + [whole()],
        out_specs=[whole()] * (1 + 2 * n_sec),
        scratch_shapes=[
            pltpu.SMEM(source.shape, jnp.int32),
            pltpu.SMEM(target.shape, jnp.int32),
            VMEM((4, rows, PANEL), BF16),
            pltpu.SemaphoreType.DMA((2,)),
            pltpu.SemaphoreType.DMA((4,)),
        ],
        input_output_aliases={2: 0},
        name="cycle",
        compiler_params=pltpu.CompilerParams(vmem_limit_bytes=24 << 20),
        cost_estimate=pl.CostEstimate(
            flops=2 * tiles.shape[0] * rows * TILE * TILE, bytes_accessed=6 << 20, transcendentals=0
        ),
    )(*in_hbm(source, target), acc, own, near, far, both, tiles)
    return outs[1 : 1 + n_sec], outs[1 + n_sec :]


def join_body(moving, kept, out):
    out[...] = (moving[...].astype(F32) + kept[...].astype(F32)).astype(out.dtype)


def join(moving, kept):
    return pl.pallas_call(
        join_body,
        out_shape=jax.ShapeDtypeStruct(moving.shape, moving.dtype),
        in_specs=[whole()] * 2,
        out_specs=whole(),
        name="join",
        compiler_params=pltpu.CompilerParams(vmem_limit_bytes=4 << 20),
        cost_estimate=pl.CostEstimate(flops=moving.size, bytes_accessed=3 << 18, transcendentals=0),
    )(moving, kept)


def columns_product(left, line, out, *, step=256):
    @pl.loop(0, line.shape[1] // step)
    def _(turn):
        cols = pl.ds(pl.multiple_of(turn * step, step), step)
        product = jnp.dot(left[...], line[:, cols], preferred_element_type=F32)
        out[:, cols] = product.astype(out.dtype)


def partner_body(left, block_0, block_1, block_2, block_3, out, line, sem):
    rows = out.shape[0]
    row = lax.axis_index("row")
    copies = []
    for d, block in enumerate((block_0, block_1, block_2, block_3)):
        at = pl.multiple_of(lax.rem(row + d, line.shape[0] // rows) * rows, rows)
        copies.append(pltpu.make_async_copy(block, line.at[pl.ds(at, rows)], sem.at[d]))
        copies[-1].start()
    for copy in copies:
        copy.wait()
    columns_product(left, line, out)


def partner_product(columns, blocks):
    rows, width = blocks[0].shape
    depth = columns.shape[1]
    return pl.pallas_call(
        partner_body,
        out_shape=(
            jax.ShapeDtypeStruct((rows, width), BF16),
            jax.ShapeDtypeStruct((depth, width), BF16),
        ),
        in_specs=[whole()] + [whole(pl.ANY)] * 4,
        out_specs=[whole()] * 2,
        scratch_shapes=[pltpu.SemaphoreType.DMA((4,))],
        name="partner",
        compiler_params=pltpu.CompilerParams(vmem_limit_bytes=10 << 20),
        cost_estimate=pl.CostEstimate(
            flops=2 * rows * depth * width, bytes_accessed=4 << 20, transcendentals=0
        ),
    )(columns, *blocks)


def own_body(hole_at, line, out, left, sem):
    depth = left.shape[1]
    row = lax.axis_index("row")
    columns = pl.ds(pl.multiple_of((row // (depth // left.shape[0])) * depth, depth), depth)
    copy = pltpu.make_async_copy(hole_at.at[:, columns], left, sem)
    copy.start()
    copy.wait()
    columns_product(left, line, out)


def own_product(hole, line):
    rows = hole.shape[0]
    depth, width = line.shape
    return pl.pallas_call(
        own_body,
        out_shape=jax.ShapeDtypeStruct((rows, width), F32),
        in_specs=[whole(pltpu.HBM), whole()],
        out_specs=whole(),
        scratch_shapes=[VMEM((rows, depth), BF16), pltpu.SemaphoreType.DMA],
        name="own",
        compiler_params=pltpu.CompilerParams(vmem_limit_bytes=10 << 20),
        cost_estimate=pl.CostEstimate(
            flops=2 * rows * depth * width, bytes_accessed=4 << 20, transcendentals=0
        ),
    )(*in_hbm(hole), line)


def base_body(
    gap_rows, gap_columns, bare, hole_own, hole_partner, low_own, low_joined, high_own, high_joined,
    out, scale,
):
    half = low_own.shape[1]
    down = jnp.broadcast_to(gap_rows[...].astype(F32), (out.shape[0], out.shape[0])).T
    for b in range(low_own.shape[0]):
        cols = slice(b * TILE, (b + 1) * TILE)
        scale[:, cols] = 1024.0 / (down + gap_columns[:, cols].astype(F32))
        both = bare[:, cols].astype(F32) + hole_own[:, cols] + hole_partner[:, cols].astype(F32)
        for u, own, joined in ((0, low_own, low_joined), (1, high_own, high_joined)):
            at = slice(u * half, (u + 1) * half)
            out[at, cols] = both[at] + own[b].astype(F32) + joined[b].astype(F32)


def base_sum(gap_rows, gap_columns, bare, hole_own, hole_partner, shares):
    rows, width = bare.shape
    out = jax.ShapeDtypeStruct((rows, width), F32)
    return pl.pallas_call(
        base_body,
        out_shape=(out, out),
        in_specs=[whole()] * 9,
        out_specs=[whole()] * 2,
        name="base",
        compiler_params=pltpu.CompilerParams(vmem_limit_bytes=10 << 20),
        cost_estimate=pl.CostEstimate(flops=5 * rows * width, bytes_accessed=4 << 20, transcendentals=0),
    )(gap_rows, gap_columns, bare, hole_own, hole_partner, *shares)


def last_body(base, scale, low, high, out_at, out, sem):
    blocks, half, _ = low.shape
    pieces = sem.shape[0]
    copies = []
    for piece in range(pieces):
        for b in range(piece * blocks // pieces, (piece + 1) * blocks // pieces):
            cols = slice(b * TILE, (b + 1) * TILE)
            for u, joined in ((0, low), (1, high)):
                at = slice(u * half, (u + 1) * half)
                residual = base[at, cols] + joined[b].astype(F32)
                out[at, cols] = (residual * scale[at, cols]).astype(out.dtype)
        width = out.shape[1] // pieces
        part = pl.ds(piece * width, width)
        copies.append(pltpu.make_async_copy(out.at[:, part], out_at.at[:, part], sem.at[piece]))
        copies[-1].start()
    for copy in copies:
        copy.wait()


def last(base, scale, low, high, *, pieces=4):
    rows, width = base.shape
    return pl.pallas_call(
        last_body,
        out_shape=jax.ShapeDtypeStruct((rows, width), BF16),
        in_specs=[whole()] * 4,
        out_specs=whole(pltpu.HBM),
        scratch_shapes=[VMEM((rows, width), BF16), pltpu.SemaphoreType.DMA((pieces,))],
        name="last",
        compiler_params=pltpu.CompilerParams(vmem_limit_bytes=8 << 20),
        cost_estimate=pl.CostEstimate(flops=3 * rows * width, bytes_accessed=3 << 20, transcendentals=0),
    )(base, scale, low, high)


def per_device(
    amplitudes,
    hole_ladder,
    bare_integrals,
    ladder_tiles,
    ladder_source,
    ladder_target,
    ladder_live,
    cycle_tiles,
    cycle_source,
    cycle_target,
    gap_rows,
    gap_columns,
    *,
    n_sec,
):
    rows = amplitudes.shape[0]
    owned = bare_integrals.shape[2]
    amps = amplitudes.reshape(rows, amplitudes.shape[2])

    forward = [(i, (i + 1) % n_sec) for i in range(n_sec)]
    backward = [(i, (i - 1) % n_sec) for i in range(n_sec)]
    core_flip = [(i, i ^ 1) for i in range(4)]
    y_flip = [(i, i ^ 2) for i in range(4)]
    row_flip = [(i, i ^ 4) for i in range(8)]
    x_next = [(i, (i & 4) + (i + 1) % 4) for i in range(8)]
    x_back = [(i, (i & 4) + (i + 3) % 4) for i in range(8)]
    x_over = [(i, (i & 4) + (i + 2) % 4) for i in range(8)]

    panel, mine, columns = prepare(amps, hole_ladder, owned)
    far = lax.ppermute(panel, "inner", y_flip)
    near = lax.ppermute(panel, "inner", core_flip)
    both = lax.ppermute(far, "inner", core_flip)
    behind = lax.ppermute(mine, "row", x_next)
    ahead = lax.ppermute(mine, "row", x_back)
    over = lax.ppermute(mine, "row", x_over)
    partner_columns = lax.ppermute(columns, "row", row_flip)

    acc = ladder(amps, ladder_tiles, ladder_source[:, 0], ladder_target[:, 0], ladder_live[:, 0])
    shares = cycle(
        acc,
        panel,
        near,
        far,
        both,
        cycle_tiles,
        cycle_source[:, 0],
        cycle_target[:, 0],
        n_sec=n_sec,
    )
    partner_part, line = partner_product(partner_columns, (mine, ahead, over, behind))
    hole_partner = lax.ppermute(partner_part, "row", row_flip)
    hole_own = own_product(hole_ladder, line)

    ends = {}
    for u in range(2):
        reach = (n_sec // 2, n_sec // 2 - 1)
        ways = (("F", forward, reach[u], 1), ("B", backward, reach[1 - u], -1))
        for name, way, hops, sign in ways:
            moving = shares[u][(sign * hops) % n_sec]
            for hop in range(hops - 1, -1, -1):
                moving = lax.ppermute(moving, "sec", way)
                if hop:
                    moving = join(moving, shares[u][(sign * hop) % n_sec])
            ends[f"{name}{u}"] = moving

    base, scale = base_sum(
        gap_rows.reshape(1, rows),
        gap_columns,
        bare_integrals.reshape(rows, owned),
        hole_own,
        hole_partner,
        (shares[0][0], ends["B0"], shares[1][0], ends["F1"]),
    )
    updated = last(base, scale, ends["F0"], ends["B1"])
    return updated.reshape(rows, 1, owned)


def solution(mesh):
    in_specs = (
        P("row", "inner", None),
        P("row", None),
        P("row", "inner", "sec"),
        P("sec", "inner", None),
        P("sec", "inner"),
        P("sec", "inner"),
        P("sec", "inner"),
        P("sec", "inner", None),
        P("sec", "inner"),
        P("sec", "inner"),
        P("row"),
        P("inner", "sec"),
    )
    out_specs = P("row", "inner", "sec")
    return jax.shard_map(
        functools.partial(per_device, n_sec=mesh.shape["sec"]),
        mesh=mesh,
        in_specs=in_specs,
        out_specs=out_specs,
        check_vma=False,
    )
```

```python
import functools

import jax
import jax.numpy as jnp
from jax import lax
from jax.experimental import pallas as pl
from jax.experimental.pallas import tpu as pltpu
from jax.sharding import PartitionSpec as P


TILE = 128
PANEL = 2048
VMEM = pltpu.VMEM
F32 = jnp.float32
BF16 = jnp.bfloat16


def whole(memory_space=VMEM):
    return pl.BlockSpec(memory_space=memory_space)


def in_hbm(*arrays):
    return tuple(pltpu.with_memory_space_constraint(a, pltpu.HBM) for a in arrays)


def panel_body(amps, panel, sem):
    copy = pltpu.make_async_copy(amps.at[:, pl.ds(0, panel.shape[1])], panel, sem)
    copy.start()
    copy.wait()


def owned_body(amps, hole, mine, columns, sem):
    wide, narrow = mine.shape[1], columns.shape[1]
    at = pl.multiple_of(lax.axis_index("sec") * wide, wide)
    line = lax.axis_index("row") // 4
    line_at = pl.multiple_of((1 - line) * narrow, narrow)
    copies = [
        pltpu.make_async_copy(amps.at[:, pl.ds(at, wide)], mine, sem.at[0]),
        pltpu.make_async_copy(hole.at[:, pl.ds(line_at, narrow)], columns, sem.at[1]),
    ]
    for copy in copies:
        copy.start()
    for copy in copies:
        copy.wait()


def picked(body, widths, *arrays):
    rows = arrays[0].shape[0]
    out = [jax.ShapeDtypeStruct((rows, width), BF16) for width in widths]
    sems = () if len(widths) == 1 else (len(widths),)
    return pl.pallas_call(
        body,
        out_shape=out,
        in_specs=[whole(pltpu.HBM)] * len(arrays),
        out_specs=[whole()] * len(out),
        scratch_shapes=[pltpu.SemaphoreType.DMA(sems)],
        compiler_params=pltpu.CompilerParams(vmem_limit_bytes=4 << 20),
        cost_estimate=pl.CostEstimate(flops=0, bytes_accessed=2 << 20, transcendentals=0),
    )(*in_hbm(*arrays))


def tile_group(turn, unroll, block_of, tiles, acc, into_of):
    products = []
    for k in range(unroll):
        slot = turn * unroll + k
        products.append(jnp.dot(block_of(slot), tiles[slot], preferred_element_type=F32))
    for k in range(unroll):
        acc[into_of(turn * unroll + k)] += products[k]


def ladder_body(
    source_at, target_at, live_at, amps_at, tiles_at, acc,
    source, target, live, amps, tiles, index_sem, amps_sem, tile_sem, *, parts, unroll,
):
    per_part = tiles.shape[0] // parts
    trash = acc.shape[0] - 1
    copies = [
        pltpu.make_async_copy(at, ref, index_sem.at[k])
        for k, (at, ref) in enumerate(
            ((source_at, source), (target_at, target), (live_at, live))
        )
    ]
    pieces = amps_sem.shape[0]
    height = amps.shape[0] // pieces
    for k in range(pieces):
        at = pl.ds(k * height, height)
        copies.append(pltpu.make_async_copy(amps_at.at[at], amps.at[at], amps_sem.at[k]))
    for copy in copies:
        copy.start()

    def tile_copy(part):
        slots = pl.ds(part * per_part, per_part)
        return pltpu.make_async_copy(tiles_at.at[slots], tiles.at[slots], tile_sem.at[part])

    tile_copy(0).start()

    @pl.loop(0, trash // 8)
    def _(block):
        acc[pl.ds(block * 8, 8)] = jnp.zeros((8,) + acc.shape[1:], F32)

    for copy in copies:
        copy.wait()
    for part in range(1, parts):
        tile_copy(part).start()

    def block_of(slot):
        return amps[:, pl.ds(pl.multiple_of(source[slot] * TILE, TILE), TILE)]

    def into_of(slot):
        return jnp.where(slot < live[0], target[slot], trash)

    for part in range(parts):
        tile_copy(part).wait()
        first = part * per_part // unroll
        count = jnp.clip(live[0] - part * per_part, 0, per_part)

        def group(turn, carry):
            tile_group(turn, unroll, block_of, tiles, acc, into_of)
            return carry

        lax.fori_loop(first, first + (count + unroll - 1) // unroll, group, 0)


def ladder(amps, tiles, source, target, live, *, parts=8, unroll=32):
    rows, width = amps.shape
    slots = tiles.shape[0]
    return pl.pallas_call(
        functools.partial(ladder_body, parts=parts, unroll=unroll),
        out_shape=jax.ShapeDtypeStruct((width // TILE + 1, rows, TILE), F32),
        in_specs=[whole(pltpu.HBM)] * 5,
        out_specs=whole(),
        scratch_shapes=[
            pltpu.SMEM(source.shape, jnp.int32),
            pltpu.SMEM(target.shape, jnp.int32),
            pltpu.SMEM(live.shape, jnp.int32),
            VMEM(amps.shape, BF16),
            VMEM(tiles.shape, BF16),
            pltpu.SemaphoreType.DMA((3,)),
            pltpu.SemaphoreType.DMA((4,)),
            pltpu.SemaphoreType.DMA((parts,)),
        ],
        name="ladder",
        compiler_params=pltpu.CompilerParams(vmem_limit_bytes=28 << 20),
        cost_estimate=pl.CostEstimate(
            flops=2 * slots * rows * TILE * TILE, bytes_accessed=12 << 20, transcendentals=0
        ),
    )(*in_hbm(source, target), live, *in_hbm(amps, tiles))


def cycle_body(
    source_at, target_at, _, own, near, far, both, tiles, acc, *rest, n_sec, unroll
):
    *shares, source, target, panels, index_sem, panel_sem = rest
    rows = acc.shape[1]
    per_panel = panels.shape[2] // TILE
    blocks, half, _ = shares[0].shape
    copies = [
        pltpu.make_async_copy(source_at, source, index_sem.at[0]),
        pltpu.make_async_copy(target_at, target, index_sem.at[1]),
    ]
    for k, panel in enumerate((own, near, far, both)):
        copies.append(pltpu.make_async_copy(panel, panels.at[k], panel_sem.at[k]))
    for copy in copies:
        copy.start()
    for copy in copies:
        copy.wait()
    sec, quarter = lax.axis_index("sec"), lax.axis_index("inner")

    def block_of(slot):
        block = source[slot]
        start = pl.multiple_of((block % per_panel) * TILE, TILE)
        return panels[(block // per_panel) ^ quarter, :, pl.ds(start, TILE)]

    def group(turn, carry):
        tile_group(turn, unroll, block_of, tiles, acc, lambda slot: target[slot])
        return carry

    lax.fori_loop(0, tiles.shape[0] // unroll, group, 0)
    for k in range(n_sec):
        chunk = lax.rem(sec + k, n_sec) * blocks
        for u in range(rows // half):
            at = pl.ds(u * half, half)
            shares[u * n_sec + k][...] = acc[pl.ds(chunk, blocks), at].astype(BF16)


def cycle(acc, own, near, far, both, tiles, source, target, *, n_sec, unroll=32):
    blocks = (acc.shape[0] - 1) // n_sec
    rows = acc.shape[1]
    share = jax.ShapeDtypeStruct((blocks, rows // 2, TILE), BF16)
    outs = pl.pallas_call(
        functools.partial(cycle_body, n_sec=n_sec, unroll=unroll),
        out_shape=(jax.ShapeDtypeStruct(acc.shape, F32),) + (share,) * (2 * n_sec),
        in_specs=[whole(pltpu.HBM)] * 2 + [whole()] + [whole(pl.ANY)] * 4 + [whole()],
        out_specs=[whole()] * (1 + 2 * n_sec),
        scratch_shapes=[
            pltpu.SMEM(source.shape, jnp.int32),
            pltpu.SMEM(target.shape, jnp.int32),
            VMEM((4, rows, PANEL), BF16),
            pltpu.SemaphoreType.DMA((2,)),
            pltpu.SemaphoreType.DMA((4,)),
        ],
        input_output_aliases={2: 0},
        name="cycle",
        compiler_params=pltpu.CompilerParams(vmem_limit_bytes=24 << 20),
        cost_estimate=pl.CostEstimate(
            flops=2 * tiles.shape[0] * rows * TILE * TILE, bytes_accessed=6 << 20, transcendentals=0
        ),
    )(*in_hbm(source, target), acc, own, near, far, both, tiles)
    return outs[1 : 1 + n_sec], outs[1 + n_sec :]


def join_body(moving, kept, out):
    out[...] = (moving[...].astype(F32) + kept[...].astype(F32)).astype(out.dtype)


def join(moving, kept):
    return pl.pallas_call(
        join_body,
        out_shape=jax.ShapeDtypeStruct(moving.shape, moving.dtype),
        in_specs=[whole()] * 2,
        out_specs=whole(),
        name="join",
        compiler_params=pltpu.CompilerParams(vmem_limit_bytes=4 << 20),
        cost_estimate=pl.CostEstimate(flops=moving.size, bytes_accessed=3 << 18, transcendentals=0),
    )(moving, kept)


def columns_product(left, line, out, *, step=256):
    @pl.loop(0, line.shape[1] // step)
    def _(turn):
        cols = pl.ds(pl.multiple_of(turn * step, step), step)
        product = jnp.dot(left[...], line[:, cols], preferred_element_type=F32)
        out[:, cols] = product.astype(out.dtype)


def partner_body(left, block_0, block_1, block_2, block_3, out, line, sem):
    rows = out.shape[0]
    row = lax.axis_index("row")
    copies = []
    for d, block in enumerate((block_0, block_1, block_2, block_3)):
        at = pl.multiple_of(lax.rem(row + d, line.shape[0] // rows) * rows, rows)
        copies.append(pltpu.make_async_copy(block, line.at[pl.ds(at, rows)], sem.at[d]))
        copies[-1].start()
    for copy in copies:
        copy.wait()
    columns_product(left, line, out)


def partner_product(columns, blocks):
    rows, width = blocks[0].shape
    depth = columns.shape[1]
    return pl.pallas_call(
        partner_body,
        out_shape=(
            jax.ShapeDtypeStruct((rows, width), BF16),
            jax.ShapeDtypeStruct((depth, width), BF16),
        ),
        in_specs=[whole()] + [whole(pl.ANY)] * 4,
        out_specs=[whole()] * 2,
        scratch_shapes=[pltpu.SemaphoreType.DMA((4,))],
        name="partner",
        compiler_params=pltpu.CompilerParams(vmem_limit_bytes=10 << 20),
        cost_estimate=pl.CostEstimate(
            flops=2 * rows * depth * width, bytes_accessed=4 << 20, transcendentals=0
        ),
    )(columns, *blocks)


def own_body(hole_at, line, out, left, sem):
    depth = left.shape[1]
    row = lax.axis_index("row")
    columns = pl.ds(pl.multiple_of((row // (depth // left.shape[0])) * depth, depth), depth)
    copy = pltpu.make_async_copy(hole_at.at[:, columns], left, sem)
    copy.start()
    copy.wait()
    columns_product(left, line, out)


def own_product(hole, line):
    rows = hole.shape[0]
    depth, width = line.shape
    return pl.pallas_call(
        own_body,
        out_shape=jax.ShapeDtypeStruct((rows, width), F32),
        in_specs=[whole(pltpu.HBM), whole()],
        out_specs=whole(),
        scratch_shapes=[VMEM((rows, depth), BF16), pltpu.SemaphoreType.DMA],
        name="own",
        compiler_params=pltpu.CompilerParams(vmem_limit_bytes=10 << 20),
        cost_estimate=pl.CostEstimate(
            flops=2 * rows * depth * width, bytes_accessed=4 << 20, transcendentals=0
        ),
    )(*in_hbm(hole), line)


def base_body(
    gap_rows, gap_columns, bare, hole_own, hole_partner, low_own, low_joined, high_own, high_joined,
    out, scale,
):
    half = low_own.shape[1]
    down = jnp.broadcast_to(gap_rows[...].astype(F32), (out.shape[0], out.shape[0])).T
    for b in range(low_own.shape[0]):
        cols = slice(b * TILE, (b + 1) * TILE)
        scale[:, cols] = 1024.0 / (down + gap_columns[:, cols].astype(F32))
        both = bare[:, cols].astype(F32) + hole_own[:, cols] + hole_partner[:, cols].astype(F32)
        for u, own, joined in ((0, low_own, low_joined), (1, high_own, high_joined)):
            at = slice(u * half, (u + 1) * half)
            out[at, cols] = both[at] + own[b].astype(F32) + joined[b].astype(F32)


def base_sum(gap_rows, gap_columns, bare, hole_own, hole_partner, shares):
    rows, width = bare.shape
    out = jax.ShapeDtypeStruct((rows, width), F32)
    return pl.pallas_call(
        base_body,
        out_shape=(out, out),
        in_specs=[whole()] * 9,
        out_specs=[whole()] * 2,
        name="base",
        compiler_params=pltpu.CompilerParams(vmem_limit_bytes=10 << 20),
        cost_estimate=pl.CostEstimate(flops=5 * rows * width, bytes_accessed=4 << 20, transcendentals=0),
    )(gap_rows, gap_columns, bare, hole_own, hole_partner, *shares)


def last_body(base, scale, low, high, out_at, out, sem):
    blocks, half, _ = low.shape
    pieces = sem.shape[0]
    copies = []
    for piece in range(pieces):
        for b in range(piece * blocks // pieces, (piece + 1) * blocks // pieces):
            cols = slice(b * TILE, (b + 1) * TILE)
            for u, joined in ((0, low), (1, high)):
                at = slice(u * half, (u + 1) * half)
                residual = base[at, cols] + joined[b].astype(F32)
                out[at, cols] = (residual * scale[at, cols]).astype(out.dtype)
        width = out.shape[1] // pieces
        part = pl.ds(piece * width, width)
        copies.append(pltpu.make_async_copy(out.at[:, part], out_at.at[:, part], sem.at[piece]))
        copies[-1].start()
    for copy in copies:
        copy.wait()


def last(base, scale, low, high, *, pieces=4):
    rows, width = base.shape
    return pl.pallas_call(
        last_body,
        out_shape=jax.ShapeDtypeStruct((rows, width), BF16),
        in_specs=[whole()] * 4,
        out_specs=whole(pltpu.HBM),
        scratch_shapes=[VMEM((rows, width), BF16), pltpu.SemaphoreType.DMA((pieces,))],
        name="last",
        compiler_params=pltpu.CompilerParams(vmem_limit_bytes=8 << 20),
        cost_estimate=pl.CostEstimate(flops=3 * rows * width, bytes_accessed=3 << 20, transcendentals=0),
    )(base, scale, low, high)


def per_device(
    amplitudes,
    hole_ladder,
    bare_integrals,
    ladder_tiles,
    ladder_source,
    ladder_target,
    ladder_live,
    cycle_tiles,
    cycle_source,
    cycle_target,
    gap_rows,
    gap_columns,
    *,
    n_sec,
):
    rows = amplitudes.shape[0]
    owned = bare_integrals.shape[2]
    amps = amplitudes.reshape(rows, amplitudes.shape[2])

    forward = [(i, (i + 1) % n_sec) for i in range(n_sec)]
    backward = [(i, (i - 1) % n_sec) for i in range(n_sec)]
    core_flip = [(i, i ^ 1) for i in range(4)]
    y_flip = [(i, i ^ 2) for i in range(4)]
    row_flip = [(i, i ^ 4) for i in range(8)]
    x_next = [(i, (i & 4) + (i + 1) % 4) for i in range(8)]
    x_back = [(i, (i & 4) + (i + 3) % 4) for i in range(8)]
    x_over = [(i, (i & 4) + (i + 2) % 4) for i in range(8)]

    (panel,) = picked(panel_body, (PANEL,), amps)
    mine, columns = picked(owned_body, (owned, 4 * rows), amps, hole_ladder)
    far = lax.ppermute(panel, "inner", y_flip)
    near = lax.ppermute(panel, "inner", core_flip)
    both = lax.ppermute(far, "inner", core_flip)
    behind = lax.ppermute(mine, "row", x_next)
    ahead = lax.ppermute(mine, "row", x_back)
    over = lax.ppermute(mine, "row", x_over)
    partner_columns = lax.ppermute(columns, "row", row_flip)

    acc = ladder(amps, ladder_tiles, ladder_source[:, 0], ladder_target[:, 0], ladder_live[:, 0])
    shares = cycle(
        acc,
        panel,
        near,
        far,
        both,
        cycle_tiles,
        cycle_source[:, 0],
        cycle_target[:, 0],
        n_sec=n_sec,
    )
    partner_part, line = partner_product(partner_columns, (mine, ahead, over, behind))
    hole_partner = lax.ppermute(partner_part, "row", row_flip)
    hole_own = own_product(hole_ladder, line)

    ends = {}
    for u in range(2):
        reach = (n_sec // 2, n_sec // 2 - 1)
        ways = (("F", forward, reach[u], 1), ("B", backward, reach[1 - u], -1))
        for name, way, hops, sign in ways:
            moving = shares[u][(sign * hops) % n_sec]
            for hop in range(hops - 1, -1, -1):
                moving = lax.ppermute(moving, "sec", way)
                if hop:
                    moving = join(moving, shares[u][(sign * hop) % n_sec])
            ends[f"{name}{u}"] = moving

    base, scale = base_sum(
        gap_rows.reshape(1, rows),
        gap_columns,
        bare_integrals.reshape(rows, owned),
        hole_own,
        hole_partner,
        (shares[0][0], ends["B0"], shares[1][0], ends["F1"]),
    )
    updated = last(base, scale, ends["F0"], ends["B1"])
    return updated.reshape(rows, 1, owned)


def solution(mesh):
    in_specs = (
        P("row", "inner", None),
        P("row", None),
        P("row", "inner", "sec"),
        P("sec", "inner", None),
        P("sec", "inner"),
        P("sec", "inner"),
        P("sec", "inner"),
        P("sec", "inner", None),
        P("sec", "inner"),
        P("sec", "inner"),
        P("row"),
        P("inner", "sec"),
    )
    out_specs = P("row", "inner", "sec")
    return jax.shard_map(
        functools.partial(per_device, n_sec=mesh.shape["sec"]),
        mesh=mesh,
        in_specs=in_specs,
        out_specs=out_specs,
        check_vma=False,
    )
```
